32 devices in a mesh: groups: 2 (over y), sub: 16 (over z, x, core).
Axes of the slice: x: 2, y: 2, z: 4, core: 2. Of those that a mesh axis runs over, the one named last changes fastest.
Arguments:
- modes: bfloat16 [65536, 512], P(('groups', 'sub')), parts along dimension 0, may hold values from -0.5 to 0.5
- eigenvalues: float32 [32, 512], P(('groups', 'sub')), parts along dimension 0, may hold values from 2 to 20
- sub_size: int32 [32], P(('groups', 'sub')), parts along dimension 0, may hold values from 1024 to 2048
- row_offset: int32 [1024, 128], P(('groups', 'sub')), parts along dimension 0, may hold values from 0 to 1023
- stiff_coupling: bfloat16 [1024, 128, 128], P(('groups', 'sub')), parts along dimension 0, may hold values from -0.29882812 to 0.29882812
- iface_offset: int32 [1024], P(('groups', 'sub')), parts along dimension 0, may hold values from 0 to 6
- stiff_iface: float32 [32, 128, 128], P(('groups', 'sub')), parts along dimension 0, may hold values from -18 to 18
- lumped_mass: float32 [32, 128], P(('groups', 'sub')), parts along dimension 0, may hold values from 0.5 to 5
Outputs:
- reduced: float32 [32, 128, 128], P(('groups', 'sub')), parts along dimension 0
- factor: float32 [32, 128, 128], P(('groups', 'sub')), parts along dimension 0
- coupled: bfloat16 [1024, 512, 128], P(('groups', 'sub')), parts along dimension 0
The draws below stay inside these ranges and needn't reach their ends.
There are 2 independent parts, one for each index of `groups`. The reference program is written for one: setup_inputs(seed, part) draws one part's arguments, and reference() takes and returns one part's arrays. A program takes and returns all parts, laid end to end along the dimension named above; each array names one. Nothing has to cross between parts.
Inputs may be any that keep to these rules, and one draw needn't show every extreme that they name: Block b of substructure s belongs to interface (s + iface_offset[b] - 3) mod 16, so a substructure's interfaces lie within 3 places of it in substructure order.
All inputs are finite; a program needn't handle non-finite values.
Results may differ from the reference program's by a relative error of at most 0.001.
The reference program's roundings to bfloat16 on the way (of `projected`) count: a program that leaves them out, or rounds other values in their place, can miss the bound.
Values sent between devices are 32-bit elements; how exact they have to be, the bound alone decides.
A program may use at most 64 MiB of HBM per device.

```python
import math
import jax
import jax.numpy as jnp
import numpy as np
from jax import lax

M = 512
IB = 128
CR = 128
NMAX = 2048
NB = 32
REACH = 3
N_SUB = 16


def with_ends(drawn, rng, low, largest):
    spot = [jax.random.randint(jax.random.fold_in(rng, axis), (), 0, length) for axis, length in enumerate(drawn.shape)]
    longest = drawn.shape.index(max(drawn.shape))
    next_to = spot[:longest] + [(spot[longest] + 1) % drawn.shape[longest]] + spot[longest + 1:]
    return drawn.at[tuple(spot)].set(low).at[tuple(next_to)].set(largest)


def block_levels(stream_key, dims, split, least, high):
    level = 1.0
    for axis_at, shards_of in split:
        draws = jax.random.uniform(jax.random.fold_in(jax.random.fold_in(stream_key, 6), axis_at), (shards_of,), jnp.float32, least / len(split), high / len(split))
        level = level * jnp.repeat(jnp.exp(draws), dims[axis_at] // shards_of).reshape((-1,) + (1,) * (len(dims) - 1 - axis_at))
    return level


def rank_table(count, lean):
    portions = [(1 << 20) // math.isqrt(standing ** lean) + 1 for standing in range(1, count + 1)]
    deviation = 1 + sum(portions) // (1 << 30)
    return np.cumsum(np.array([max(1, weight // deviation) for weight in portions]))


def skewed_ids(stream_key, extent, number_of, skew):
    table = rank_table(number_of, skew)
    pick = jax.random.randint(jax.random.fold_in(stream_key, 1), extent, 0, int(table[number_of - 1]))
    standing = jnp.searchsorted(jnp.asarray(table, jnp.int32), pick, side="right")
    return jax.random.permutation(jax.random.fold_in(stream_key, 2), number_of)[standing].astype(jnp.int32)


def bell_draw(stream_key, dims, width, limit, shards=(), held_as=jnp.bfloat16):
    values = jax.random.normal(stream_key, dims, jnp.float32) * width
    if len(shards) > 0:
        values = block_levels(stream_key, dims, shards, -0.22, 0.18) * values
    return jnp.clip(values, min=-limit, max=limit).astype(held_as)


def setup_inputs(seed: int = 0, part: int = 0) -> dict:
    arg_keys = jax.random.split(jax.random.key(seed), 9)
    part_splits = jax.random.split(jax.random.fold_in(arg_keys[8], part), 9)
    modes = bell_draw(part_splits[0], (N_SUB * NMAX, M), CR ** -0.5, 0.5, ((0, 16),))
    eigenvalues = jnp.clip(jnp.exp(math.log(20.0) - 2.3025851 * jax.random.uniform(part_splits[1], (N_SUB, M), jnp.float32) ** block_levels(part_splits[1], (N_SUB, M), ((0, 16),), -0.2, 0.2)), 2.0, 20.0)
    sub_size = with_ends(jax.random.randint(part_splits[2], (N_SUB,), NMAX // 2, NMAX + 1), jax.random.fold_in(part_splits[2], 1), NMAX // 2, NMAX).astype(jnp.int32)
    row_offset = with_ends(jax.random.randint(part_splits[3], (N_SUB * NB, CR), 0, NMAX // 2), jax.random.fold_in(part_splits[3], 1), 0, (NMAX // 2) - 1).astype(jnp.int32)
    stiff_coupling = bell_draw(part_splits[4], (N_SUB * NB, CR, IB), 0.05, 0.29882812, ((0, 16),))
    iface_offset = with_ends(skewed_ids(part_splits[5], (N_SUB * NB,), 2 * REACH + 1, 2), jax.random.fold_in(part_splits[5], 3), 0, 2 * REACH).astype(jnp.int32)
    stiff_iface = bell_draw(part_splits[6], (N_SUB, IB, IB), 3.0, 18.0, ((0, 16),), jnp.float32)
    lumped_mass = jnp.clip(jnp.exp(math.log(5.0) - 2.3025851 * jax.random.uniform(part_splits[7], (N_SUB, IB), jnp.float32) ** block_levels(part_splits[7], (N_SUB, IB), ((0, 16),), -0.2, 0.2)), 0.5, 5.0)
    return {"modes": modes, "eigenvalues": eigenvalues, "sub_size": sub_size, "row_offset": row_offset, "stiff_coupling": stiff_coupling, "iface_offset": iface_offset, "stiff_iface": stiff_iface, "lumped_mass": lumped_mass}


def project(modes_block, size_value, offsets, coupling):
    picked_rows = (size_value - 1 - offsets).astype(jnp.int32)
    picked = jnp.take(modes_block, picked_rows, axis=0).astype(jnp.float32)
    return jnp.einsum('brm,bri->bmi', picked, coupling.astype(jnp.float32)).astype(jnp.bfloat16)

def schur_terms(projected, eigen_row):
    widened = projected.astype(jnp.float32)
    inverse = 1.0 / eigen_row
    stiff_part = jnp.einsum('bmi,bmj->bij', widened * inverse[None, :, None], widened, precision=lax.Precision.HIGHEST)
    mass_part = jnp.einsum('bmi,bmj->bij', widened * (inverse * inverse)[None, :, None], widened, precision=lax.Precision.HIGHEST)
    return (stiff_part, mass_part)

def reference(modes, eigenvalues, sub_size, row_offset, stiff_coupling, iface_offset, stiff_iface, lumped_mass):
    modes_all = modes.reshape(N_SUB, NMAX, M)
    offsets_all = row_offset.reshape(N_SUB, NB, CR)
    coupling_all = stiff_coupling.reshape(N_SUB, NB, CR, IB)
    owners_row = jnp.arange(N_SUB, dtype=jnp.int32)[:, None]
    targets = ((iface_offset.reshape(N_SUB, NB) - REACH + owners_row) % N_SUB).astype(jnp.int32)

    def accumulate(totals, inputs):
        modes_block, size_value, offsets, coupling, eigen_row, target_row = inputs
        projected = project(modes_block, size_value, offsets, coupling)
        stiff_part, mass_part = schur_terms(projected, eigen_row)
        return ((totals[0].at[target_row].add(stiff_part), totals[1].at[target_row].add(mass_part)), None)
    zeros_block = jnp.zeros((N_SUB, IB, IB), jnp.float32)
    (stiff_sum, mass_sum), _ = lax.scan(accumulate, (zeros_block, zeros_block), (modes_all, sub_size, offsets_all, coupling_all, eigenvalues, targets))
    reduced = stiff_iface - stiff_sum
    identity = jnp.eye(IB, dtype=jnp.float32)
    mass_matrix = mass_sum + lumped_mass[:, :, None] * identity[None]
    factor = jnp.linalg.cholesky(mass_matrix)
    inverse_factor = lax.linalg.triangular_solve(factor, jnp.broadcast_to(identity, factor.shape), left_side=True, lower=True)

    def transform(inputs):
        modes_block, size_value, offsets, coupling, target_row = inputs
        projected = project(modes_block, size_value, offsets, coupling).astype(jnp.float32)
        chosen = inverse_factor[target_row]
        solved = jnp.einsum('bmi,bji->bmj', projected, chosen, precision=lax.Precision.HIGHEST)
        return solved.astype(jnp.bfloat16)
    coupled = lax.map(transform, (modes_all, sub_size, offsets_all, coupling_all, targets))
    return (reduced, factor, coupled.reshape(N_SUB * NB, M, IB))
```

```python
import functools

import jax
import jax.numpy as jnp
from jax import lax
from jax.experimental import pallas as pl
from jax.experimental.pallas import tpu as pltpu
from jax.sharding import PartitionSpec as P

REACH = 3
SPOTS = 2 * REACH + 1
GROUP = 4
PANEL = 8
MESH_ID = pl.DeviceIdType.MESH
HIGHEST = lax.Precision.HIGHEST


def dot(a, b, over_a=1, over_b=0, precision=None):
    return lax.dot_general(
        a,
        b,
        (((over_a,), (over_b,)), ((), ())),
        precision=precision,
        preferred_element_type=jnp.float32,
    )


def in_two(x):
    high = x.astype(jnp.bfloat16)
    low = (x - high.astype(jnp.float32)).astype(jnp.bfloat16)
    return high, low


def project_kernel(
    size_ref, spot_ref, modes_ref, eig_ref, offset_ref, coupling_ref,
    projected_ref, stiff_ref, mass_ref, window_ref, inverse_ref,
):
    step = pl.program_id(0)
    half = modes_ref.shape[0] // 2
    width = coupling_ref.shape[2]
    depth = coupling_ref.shape[1]
    count = modes_ref.shape[1]
    size = size_ref[0]

    @pl.when(step == 0)
    def _():
        spots = lax.broadcasted_iota(jnp.int32, (half, count), 0)
        window = jnp.where(
            spots + half < size,
            modes_ref[half:, :].astype(jnp.float32),
            modes_ref[:half, :].astype(jnp.float32),
        )
        window_ref[...] = jnp.transpose(window).astype(jnp.bfloat16)
        inverse_ref[...] = jnp.transpose(
            jnp.broadcast_to(1.0 / eig_ref[...], (width, count))
        )
        stiff_ref[...] = jnp.zeros_like(stiff_ref)
        mass_ref[...] = jnp.zeros_like(mass_ref)

    inverse = inverse_ref[...]
    for pair in range(GROUP // 2):
        hot = []
        for block in (2 * pair, 2 * pair + 1):
            row = size - 1 - offset_ref[pl.ds(step * GROUP + block, 1), :]
            row = jnp.where(row >= half, row - half, row)
            spots = lax.broadcasted_iota(jnp.int32, (half, depth), 0)
            hot.append(jnp.where(spots == row, 1.0, 0.0).astype(jnp.bfloat16))
        picked = dot(window_ref[...], jnp.concatenate(hot, axis=1)).astype(jnp.bfloat16)
        for place in range(2):
            block = 2 * pair + place
            projected = dot(
                picked[:, place * depth:(place + 1) * depth], coupling_ref[block]
            ).astype(jnp.bfloat16)
            projected_ref[block] = projected
            once = projected.astype(jnp.float32) * inverse
            twice = once * inverse
            once_high, once_low = in_two(once)
            twice_high, twice_low = in_two(twice)
            turned = jnp.transpose(projected)
            terms = dot(turned, jnp.concatenate([once_high, twice_high], axis=1)) + dot(
                turned, jnp.concatenate([once_low, twice_low], axis=1)
            )
            spot = spot_ref[step * GROUP + block]
            stiff_ref[spot] += terms[:, :width]
            mass_ref[spot] += terms[:, width:]


def factor_rows(work_ref, rows_ref):
    width = work_ref.shape[0]

    def panel(at, carry):
        base = pl.multiple_of(at * PANEL, PANEL)
        block = work_ref[pl.ds(base, PANEL), :]
        ahead = pltpu.roll(block[:, :width], width - base, 1)
        entry = {}
        for i in range(PANEL):
            for j in range(i + 1):
                entry[i, j] = jnp.broadcast_to(ahead[j:j + 1, i:i + 1], (1, width))
        rows = [[block[i:i + 1, :width], block[i:i + 1, width:]] for i in range(PANEL)]
        for k in range(PANEL):
            pivot = entry[k, k]
            root = lax.rsqrt(pivot)
            root = root * (1.5 - 0.5 * pivot * root * root)
            for i in range(k + 1, PANEL):
                entry[i, k] = entry[i, k] * root
            rows[k] = [x * root for x in rows[k]]
            for i in range(k + 1, PANEL):
                for j in range(k + 1, i + 1):
                    entry[i, j] = entry[i, j] - entry[i, k] * entry[j, k]
                rows[i] = [x - entry[i, k] * y for x, y in zip(rows[i], rows[k])]
        done = jnp.concatenate(
            [jnp.concatenate([x[0] for x in rows], axis=0), jnp.concatenate([x[1] for x in rows], axis=0)],
            axis=1,
        )
        rows_ref[pl.ds(base, PANEL), :] = done
        work_ref[...] = work_ref[...] - dot(jnp.transpose(done[:, :width]), done, precision=HIGHEST)
        return carry

    lax.fori_loop(0, width // PANEL, panel, 0)


def exchange_kernel(
    stiff_ref, mass_ref, iface_ref, lumped_ref, reduced_ref, factor_ref, near_ref,
    stiff_in, mass_in, near_in, own_ref, work_ref, rows_ref, send_sem, recv_sem,
):
    length = lax.axis_size("sub")
    me = lax.axis_index("sub")
    width = lumped_ref.shape[1]
    others = [d for d in (-3, 3, -2, 2, -1, 1)]

    def device(by):
        return lax.rem(me + by + length, length)

    barrier = pltpu.get_barrier_semaphore()
    for d in others:
        pl.semaphore_signal(barrier, inc=1, device_id={"sub": device(d)}, device_id_type=MESH_ID)
    pl.semaphore_wait(barrier, len(others))

    def send(kind, source, landing, by, slot):
        copy = pltpu.make_async_remote_copy(
            src_ref=source,
            dst_ref=landing.at[slot],
            send_sem=send_sem.at[kind, slot],
            recv_sem=recv_sem.at[kind, slot],
            device_id={"sub": device(by)},
            device_id_type=MESH_ID,
        )
        copy.start()
        return copy

    mass_copies = [send(0, mass_ref.at[d + REACH], mass_in, d, d + REACH) for d in others]
    stiff_copies = [send(1, stiff_ref.at[d + REACH], stiff_in, d, d + REACH) for d in others]
    across = lax.broadcasted_iota(jnp.int32, (width, width), 0)
    along = lax.broadcasted_iota(jnp.int32, (width, width), 1)
    for copy in mass_copies:
        copy.wait_recv()
    mass = mass_ref[REACH]
    for d in others:
        mass = mass + mass_in[d + REACH]
    mass = mass + jnp.where(across == along, lumped_ref[...], 0.0)
    work_ref[:, :width] = mass
    work_ref[:, width:] = jnp.where(across == along, 1.0, 0.0)
    factor_rows(work_ref, rows_ref)
    own_ref[...] = jnp.transpose(jnp.where(across >= along, rows_ref[:, width:], 0.0))
    factor_ref[...] = jnp.transpose(jnp.where(across <= along, rows_ref[:, :width], 0.0))
    near_copies = [send(2, own_ref, near_in, -d, d + REACH) for d in others]
    for copy in stiff_copies:
        copy.wait_recv()
    stiff = stiff_ref[REACH]
    for d in others:
        stiff = stiff + stiff_in[d + REACH]
    reduced_ref[...] = iface_ref[0] - stiff
    for copy in mass_copies + stiff_copies:
        copy.wait_send()

    def place(slot, x):
        high, low = in_two(x)
        near_ref[slot, :width, :] = high
        near_ref[slot, width:, :] = low

    place(REACH, own_ref[...])
    for copy in near_copies:
        copy.wait()
    for d in others:
        place(d + REACH, near_in[d + REACH])


def couple_kernel(
    spot_ref, projected_ref, near_ref, reduced_in, factor_in, coupled_ref, reduced_ref, factor_ref
):
    step = pl.program_id(0)

    @pl.when(step == 0)
    def _():
        reduced_ref[0] = reduced_in[...]
        factor_ref[0] = factor_in[...]

    for block in range(GROUP):
        x = projected_ref[block]
        coupled_ref[block] = dot(
            jnp.concatenate([x, x], axis=1), near_ref[spot_ref[step * GROUP + block]]
        ).astype(jnp.bfloat16)


def per_device(
    modes, eigenvalues, sub_size, row_offset, stiff_coupling, iface_offset, stiff_iface, lumped_mass
):
    blocks, depth, width = stiff_coupling.shape
    most, count = modes.shape
    f32, bf16 = jnp.float32, jnp.bfloat16
    full = lambda *shape: pl.BlockSpec(shape, lambda i, *_: (0,) * len(shape))
    projected, stiff, mass = pl.pallas_call(
        project_kernel,
        grid_spec=pltpu.PrefetchScalarGridSpec(
            num_scalar_prefetch=2,
            grid=(blocks // GROUP,),
            in_specs=[
                full(most, count),
                full(1, count),
                full(blocks, depth),
                pl.BlockSpec((GROUP, depth, width), lambda i, *_: (i, 0, 0)),
            ],
            out_specs=[
                pl.BlockSpec((GROUP, count, width), lambda i, *_: (i, 0, 0)),
                full(SPOTS, width, width),
                full(SPOTS, width, width),
            ],
            scratch_shapes=[
                pltpu.VMEM((count, most // 2), bf16),
                pltpu.VMEM((count, width), f32),
            ],
        ),
        out_shape=[
            jax.ShapeDtypeStruct((blocks, count, width), bf16),
            jax.ShapeDtypeStruct((SPOTS, width, width), f32),
            jax.ShapeDtypeStruct((SPOTS, width, width), f32),
        ],
        compiler_params=pltpu.CompilerParams(dimension_semantics=("arbitrary",)),
        name="project",
    )(sub_size, iface_offset, modes, eigenvalues, row_offset, stiff_coupling)

    vmem = pl.BlockSpec(memory_space=pltpu.VMEM)
    reduced, factor, near = pl.pallas_call(
        exchange_kernel,
        in_specs=[vmem] * 4,
        out_specs=[vmem] * 3,
        out_shape=[
            jax.ShapeDtypeStruct((width, width), f32),
            jax.ShapeDtypeStruct((width, width), f32),
            jax.ShapeDtypeStruct((SPOTS, 2 * width, width), bf16),
        ],
        scratch_shapes=[
            pltpu.VMEM((SPOTS, width, width), f32),
            pltpu.VMEM((SPOTS, width, width), f32),
            pltpu.VMEM((SPOTS, width, width), f32),
            pltpu.VMEM((width, width), f32),
            pltpu.VMEM((width, 2 * width), f32),
            pltpu.VMEM((width, 2 * width), f32),
            pltpu.SemaphoreType.DMA((3, SPOTS)),
            pltpu.SemaphoreType.DMA((3, SPOTS)),
        ],
        compiler_params=pltpu.CompilerParams(collective_id=0, has_side_effects=True),
        name="exchange",
    )(stiff, mass, stiff_iface, lumped_mass)

    coupled, reduced, factor = pl.pallas_call(
        couple_kernel,
        grid_spec=pltpu.PrefetchScalarGridSpec(
            num_scalar_prefetch=1,
            grid=(blocks // GROUP,),
            in_specs=[
                pl.BlockSpec((GROUP, count, width), lambda i, *_: (i, 0, 0)),
                full(SPOTS, 2 * width, width),
                full(width, width),
                full(width, width),
            ],
            out_specs=[
                pl.BlockSpec((GROUP, count, width), lambda i, *_: (i, 0, 0)),
                full(1, width, width),
                full(1, width, width),
            ],
        ),
        out_shape=[
            jax.ShapeDtypeStruct((blocks, count, width), bf16),
            jax.ShapeDtypeStruct((1, width, width), f32),
            jax.ShapeDtypeStruct((1, width, width), f32),
        ],
        compiler_params=pltpu.CompilerParams(dimension_semantics=("arbitrary",)),
        name="couple",
    )(iface_offset, projected, near, reduced, factor)
    return reduced, factor, coupled


def solution(mesh):
    placed = (
        P(("groups", "sub"), None),
        P(("groups", "sub"), None),
        P(("groups", "sub")),
        P(("groups", "sub"), None),
        P(("groups", "sub"), None, None),
        P(("groups", "sub")),
        P(("groups", "sub"), None, None),
        P(("groups", "sub"), None),
    )
    return jax.shard_map(
        per_device,
        mesh=mesh,
        in_specs=placed,
        out_specs=(
            P(("groups", "sub"), None, None),
            P(("groups", "sub"), None, None),
            P(("groups", "sub"), None, None),
        ),
        check_vma=False,
    )
```

```python
import functools

import jax
import jax.numpy as jnp
from jax import lax
from jax.experimental import pallas as pl
from jax.experimental.pallas import tpu as pltpu
from jax.sharding import PartitionSpec as P

REACH = 3
SPOTS = 2 * REACH + 1
GROUP = 4
PANEL = 8
PIECES = 4
MESH_ID = pl.DeviceIdType.MESH
HIGHEST = lax.Precision.HIGHEST


def dot(a, b, over_a=1, over_b=0, precision=None):
    return lax.dot_general(
        a,
        b,
        (((over_a,), (over_b,)), ((), ())),
        precision=precision,
        preferred_element_type=jnp.float32,
    )


def in_two(x):
    high = x.astype(jnp.bfloat16)
    low = (x - high.astype(jnp.float32)).astype(jnp.bfloat16)
    return high, low


def project_kernel(
    size_ref, spot_ref, offset_ref, modes_ref, eig_ref, coupling_ref,
    projected_ref, stiff_ref, packed_ref, mass_ref, rows_ref, inverse_ref, first_ref, start_ref, sem, *picked_refs,
):
    step = pl.program_id(0)
    depth, width = coupling_ref.shape[1:]
    most, count = modes_ref.shape
    parts = count // width
    blocks = offset_ref.shape[0]

    def gather(at, into, low, high):
        for r in range(low, high):
            into[pl.ds(r * parts, parts), :] = rows_ref[pl.ds(start_ref[at, r], parts), :]

    @pl.when(step == 0)
    def _():
        first_ref[...] = (size_ref[0] - 1 - offset_ref[...]) * parts
        for chunk in range(parts):
            rows_ref[pl.ds(chunk, most, stride=parts), :] = modes_ref[
                :, chunk * width:(chunk + 1) * width
            ].astype(jnp.float32)
            if chunk == 0:
                starts = pltpu.make_async_copy(first_ref, start_ref, sem)
                starts.start()
        inverse_ref[...] = 1.0 / jnp.broadcast_to(eig_ref[...], inverse_ref.shape)
        stiff_ref[...] = jnp.zeros_like(stiff_ref)
        mass_ref[...] = jnp.zeros_like(mass_ref)
        starts.wait()
        gather(0, picked_refs[0], 0, depth)

    for block in range(GROUP):
        at = step * GROUP + block
        following = jnp.minimum(at + 1, blocks - 1)
        into = picked_refs[(block + 1) % GROUP]
        source = picked_refs[block]
        picked = jnp.concatenate(
            [source[pl.ds(chunk, depth, stride=parts), :].astype(jnp.bfloat16) for chunk in range(parts)],
            axis=1,
        )
        gather(following, into, 0, depth // 2)
        turned = dot(jnp.transpose(coupling_ref[block]), picked).astype(jnp.bfloat16)
        projected_ref[block] = jnp.transpose(turned)
        gather(following, into, depth // 2, depth)
        inverse = inverse_ref[...]
        wide = turned.astype(jnp.float32)
        once = wide * inverse
        twice = once * inverse
        once_high, once_low = in_two(once)
        twice_high, twice_low = in_two(twice)
        high = jnp.concatenate([once_high, twice_high], axis=0)
        low = jnp.concatenate([once_low, twice_low], axis=0)
        terms = dot(turned, high, 1, 1) + dot(turned, low, 1, 1)
        spot = spot_ref[at]
        stiff_ref[spot] += terms[:, :width]
        mass_ref[spot] += terms[:, width:]

    @pl.when(step == pl.num_programs(0) - 1)
    def _():
        half = width // 2
        across = lax.broadcasted_iota(jnp.int32, (half, width), 0)
        along = lax.broadcasted_iota(jnp.int32, (half, width), 1)
        for slot in range(SPOTS):
            moved = pltpu.roll(mass_ref[slot, half:, :], half, 1)
            packed_ref[slot, :half, :] = jnp.where(along < across, moved, mass_ref[slot, :half, :])
            diagonal = jnp.sum(jnp.where(along == across, moved, 0.0), axis=0, keepdims=True)
            packed_ref[slot, half:, :] = jnp.broadcast_to(diagonal, (PANEL, width))


def factor_rows(work_ref, rows_ref, first, last):
    width = work_ref.shape[0]

    def panel(at, carry):
        base = pl.multiple_of(at * PANEL, PANEL)
        block = work_ref[pl.ds(base, PANEL), :]
        ahead = pltpu.roll(block[:, :width], width - base, 1)
        entry = {}
        for i in range(PANEL):
            for j in range(i + 1):
                entry[i, j] = jnp.broadcast_to(ahead[j:j + 1, i:i + 1], (1, width))
        rows = [[block[i:i + 1, :width], block[i:i + 1, width:]] for i in range(PANEL)]
        for k in range(PANEL):
            pivot = entry[k, k]
            root = lax.rsqrt(pivot)
            root = root * (1.5 - 0.5 * pivot * root * root)
            for i in range(k + 1, PANEL):
                entry[i, k] = entry[i, k] * root
            rows[k] = [x * root for x in rows[k]]
            for i in range(k + 1, PANEL):
                for j in range(k + 1, i + 1):
                    entry[i, j] = entry[i, j] - entry[i, k] * entry[j, k]
                rows[i] = [x - entry[i, k] * y for x, y in zip(rows[i], rows[k])]
        done = jnp.concatenate(
            [jnp.concatenate([x[0] for x in rows], axis=0), jnp.concatenate([x[1] for x in rows], axis=0)],
            axis=1,
        )
        rows_ref[pl.ds(base, PANEL), :] = done
        work_ref[...] = work_ref[...] - dot(jnp.transpose(done[:, :width]), done, precision=HIGHEST)
        return carry

    lax.fori_loop(first // PANEL, last // PANEL, panel, 0)


def exchange_kernel(
    stiff_ref, mass_ref, iface_ref, lumped_ref, reduced_ref, factor_ref, near_ref,
    stiff_in, mass_in, near_in, own_ref, work_ref, rows_ref, send_sem, recv_sem, local_sem,
):
    length = lax.axis_size("sub")
    me = lax.axis_index("sub")
    width = lumped_ref.shape[1]
    half = width // 2
    others = (-3, 3, -2, 2, -1, 1)

    def device(by):
        return lax.rem(me + by + length, length)

    own_mass = pltpu.make_async_copy(mass_ref.at[REACH], mass_in.at[REACH], local_sem.at[0])
    own_stiff = pltpu.make_async_copy(stiff_ref.at[REACH], stiff_in.at[REACH], local_sem.at[1])
    own_mass.start()
    own_stiff.start()
    barrier = pltpu.get_barrier_semaphore()
    for d in others:
        pl.semaphore_signal(barrier, inc=1, device_id={"sub": device(d)}, device_id_type=MESH_ID)
    pl.semaphore_wait(barrier, len(others))

    def send(kind, source, landing, by, slot):
        copy = pltpu.make_async_remote_copy(
            src_ref=source,
            dst_ref=landing,
            send_sem=send_sem.at[kind, slot],
            recv_sem=recv_sem.at[kind, slot],
            device_id={"sub": device(by)},
            device_id_type=MESH_ID,
        )
        copy.start()
        return copy

    mass_copies = [
        send(0, mass_ref.at[d + REACH], mass_in.at[d + REACH], d, d + REACH) for d in others
    ]
    across = lax.broadcasted_iota(jnp.int32, (width, width), 0)
    along = lax.broadcasted_iota(jnp.int32, (width, width), 1)
    own_mass.wait()
    for copy in mass_copies:
        copy.wait_recv()
    stiff_copies = [
        send(1, stiff_ref.at[d + REACH], stiff_in.at[d + REACH], d, d + REACH) for d in others
    ]
    packed = mass_in[REACH]
    for d in others:
        packed = packed + mass_in[d + REACH]
    top = packed[:half]
    low = jnp.concatenate([jnp.zeros_like(top), pltpu.roll(top, half, 1)], axis=0)
    low = jnp.transpose(jnp.where((across >= half) & (along >= half) & (along < across), low, 0.0))
    diagonal = pltpu.roll(packed[half:half + 1], half, 1)
    bottom = jnp.where(across[half:] == along[half:], diagonal, low[half:])
    mass = jnp.concatenate([top, bottom], axis=0)
    work_ref[:, :width] = jnp.where(across == along, mass + lumped_ref[...], mass)
    work_ref[:, width:] = jnp.where(across == along, 1.0, 0.0)
    near_copies = []
    rows = width // PIECES
    for piece in range(PIECES):
        part = pl.ds(piece * rows, rows)
        factor_rows(work_ref, rows_ref, piece * rows, (piece + 1) * rows)
        begun = slice(piece * rows, (piece + 1) * rows)
        own_ref[part, :] = jnp.where(across[begun] >= along[begun], rows_ref[part, width:], 0.0)
        near_copies += [
            send(2 + piece, own_ref.at[part], near_in.at[d + REACH, part], -d, d + REACH) for d in others
        ]
    factor_ref[...] = jnp.transpose(jnp.where(across <= along, rows_ref[:, :width], 0.0))
    own_stiff.wait()
    for copy in stiff_copies:
        copy.wait_recv()
    stiff = stiff_in[REACH]
    for d in others:
        stiff = stiff + stiff_in[d + REACH]
    reduced_ref[...] = iface_ref[0] - stiff
    for copy in mass_copies + stiff_copies:
        copy.wait_send()

    def place(slot, x):
        high, low = in_two(x)
        near_ref[slot, :, :width] = high
        near_ref[slot, :, width:] = low

    place(REACH, own_ref[...])
    for copy in near_copies:
        copy.wait()
    for d in others:
        place(d + REACH, near_in[d + REACH])


def couple_kernel(
    spot_ref, projected_ref, near_ref, reduced_in, factor_in, coupled_ref, reduced_ref, factor_ref
):
    step = pl.program_id(0)

    @pl.when(step == 0)
    def _():
        reduced_ref[0] = reduced_in[...]
        factor_ref[0] = factor_in[...]

    for block in range(GROUP):
        x = projected_ref[block]
        coupled_ref[block] = dot(
            jnp.concatenate([x, x], axis=1), near_ref[spot_ref[step * GROUP + block]], 1, 1
        ).astype(jnp.bfloat16)


def per_device(
    modes, eigenvalues, sub_size, row_offset, stiff_coupling, iface_offset, stiff_iface, lumped_mass
):
    blocks, depth, width = stiff_coupling.shape
    most, count = modes.shape
    f32, bf16 = jnp.float32, jnp.bfloat16
    full = lambda *shape: pl.BlockSpec(shape, lambda i, *_: (0,) * len(shape))
    projected, stiff, mass = pl.pallas_call(
        project_kernel,
        grid_spec=pltpu.PrefetchScalarGridSpec(
            num_scalar_prefetch=2,
            grid=(blocks // GROUP,),
            in_specs=[
                full(blocks, depth),
                full(most, count),
                full(1, count),
                pl.BlockSpec((GROUP, depth, width), lambda i, *_: (i, 0, 0)),
            ],
            out_specs=[
                pl.BlockSpec((GROUP, count, width), lambda i, *_: (i, 0, 0)),
                full(SPOTS, width, width),
                full(SPOTS, width // 2 + PANEL, width),
            ],
            scratch_shapes=[
                pltpu.VMEM((SPOTS, width, width), f32),
                pltpu.VMEM((most * count // width, width), f32),
                pltpu.VMEM((width, count), f32),
                pltpu.VMEM((blocks, depth), jnp.int32),
                pltpu.SMEM((blocks, depth), jnp.int32),
                pltpu.SemaphoreType.DMA,
            ]
            + [pltpu.VMEM((depth * count // width, width), f32)] * GROUP,
        ),
        out_shape=[
            jax.ShapeDtypeStruct((blocks, count, width), bf16),
            jax.ShapeDtypeStruct((SPOTS, width, width), f32),
            jax.ShapeDtypeStruct((SPOTS, width // 2 + PANEL, width), f32),
        ],
        compiler_params=pltpu.CompilerParams(dimension_semantics=("arbitrary",)),
        name="project",
    )(sub_size, iface_offset, row_offset, modes, eigenvalues, stiff_coupling)

    vmem = pl.BlockSpec(memory_space=pltpu.VMEM)
    reduced, factor, near = pl.pallas_call(
        exchange_kernel,
        in_specs=[pl.BlockSpec(memory_space=pl.ANY)] * 2 + [vmem] * 2,
        out_specs=[vmem] * 3,
        out_shape=[
            jax.ShapeDtypeStruct((width, width), f32),
            jax.ShapeDtypeStruct((width, width), f32),
            jax.ShapeDtypeStruct((SPOTS, width, 2 * width), bf16),
        ],
        scratch_shapes=[
            pltpu.VMEM((SPOTS, width, width), f32),
            pltpu.VMEM((SPOTS, width // 2 + PANEL, width), f32),
            pltpu.VMEM((SPOTS, width, width), f32),
            pltpu.VMEM((width, width), f32),
            pltpu.VMEM((width, 2 * width), f32),
            pltpu.VMEM((width, 2 * width), f32),
            pltpu.SemaphoreType.DMA((2 + PIECES, SPOTS)),
            pltpu.SemaphoreType.DMA((2 + PIECES, SPOTS)),
            pltpu.SemaphoreType.DMA((2,)),
        ],
        compiler_params=pltpu.CompilerParams(collective_id=0, has_side_effects=True),
        name="exchange",
    )(stiff, mass, stiff_iface, lumped_mass)

    coupled, reduced, factor = pl.pallas_call(
        couple_kernel,
        grid_spec=pltpu.PrefetchScalarGridSpec(
            num_scalar_prefetch=1,
            grid=(blocks // GROUP,),
            in_specs=[
                pl.BlockSpec((GROUP, count, width), lambda i, *_: (i, 0, 0)),
                full(SPOTS, width, 2 * width),
                full(width, width),
                full(width, width),
            ],
            out_specs=[
                pl.BlockSpec((GROUP, count, width), lambda i, *_: (i, 0, 0)),
                full(1, width, width),
                full(1, width, width),
            ],
        ),
        out_shape=[
            jax.ShapeDtypeStruct((blocks, count, width), bf16),
            jax.ShapeDtypeStruct((1, width, width), f32),
            jax.ShapeDtypeStruct((1, width, width), f32),
        ],
        compiler_params=pltpu.CompilerParams(dimension_semantics=("arbitrary",)),
        name="couple",
    )(iface_offset, projected, near, reduced, factor)
    return reduced, factor, coupled


def solution(mesh):
    placed = (
        P(("groups", "sub"), None),
        P(("groups", "sub"), None),
        P(("groups", "sub")),
        P(("groups", "sub"), None),
        P(("groups", "sub"), None, None),
        P(("groups", "sub")),
        P(("groups", "sub"), None, None),
        P(("groups", "sub"), None),
    )
    return jax.shard_map(
        per_device,
        mesh=mesh,
        in_specs=placed,
        out_specs=(
            P(("groups", "sub"), None, None),
            P(("groups", "sub"), None, None),
            P(("groups", "sub"), None, None),
        ),
        check_vma=False,
    )
```

```python
import functools

import jax
import jax.numpy as jnp
from jax import lax
from jax.experimental import pallas as pl
from jax.experimental.pallas import tpu as pltpu
from jax.sharding import PartitionSpec as P

REACH = 3
SPOTS = 2 * REACH + 1
GROUP = 4
PANEL = 8
PIECES = 4
MESH_ID = pl.DeviceIdType.MESH
MIB = 1 << 20


def dot(a, b, over_a=1, over_b=0):
    return lax.dot_general(
        a,
        b,
        (((over_a,), (over_b,)), ((), ())),
        preferred_element_type=jnp.float32,
    )


def in_two(x):
    high = x.astype(jnp.bfloat16)
    low = (x - high.astype(jnp.float32)).astype(jnp.bfloat16)
    return high, low


def in_three(x):
    high = x.astype(jnp.bfloat16).astype(jnp.float32)
    middle = (x - high).astype(jnp.bfloat16).astype(jnp.float32)
    return high, middle, x - high - middle


def project_kernel(
    size_ref, spot_ref, offset_ref, modes_ref, eig_ref, coupling_ref,
    projected_ref, stiff_ref, packed_ref, mass_ref, rows_ref, inverse_ref, first_ref, start_ref, sem, *picked_refs,
):
    step = pl.program_id(0)
    depth, width = coupling_ref.shape[1:]
    most, count = modes_ref.shape
    parts = count // width
    blocks = offset_ref.shape[0]

    def gather(at, into, low, high):
        for r in range(low, high):
            into[pl.ds(r * parts, parts), :] = rows_ref[pl.ds(start_ref[at, r], parts), :]

    @pl.when(step == 0)
    def _():
        first_ref[...] = (size_ref[0] - 1 - offset_ref[...]) * parts
        for chunk in range(parts):
            rows_ref[pl.ds(chunk, most, stride=parts), :] = modes_ref[
                :, chunk * width:(chunk + 1) * width
            ].astype(jnp.float32)
            if chunk == 0:
                starts = pltpu.make_async_copy(first_ref, start_ref, sem)
                starts.start()
        inverse_ref[...] = 1.0 / jnp.broadcast_to(eig_ref[...], inverse_ref.shape)
        stiff_ref[...] = jnp.zeros_like(stiff_ref)
        mass_ref[...] = jnp.zeros_like(mass_ref)
        starts.wait()
        gather(0, picked_refs[0], 0, depth)

    for block in range(GROUP):
        at = step * GROUP + block
        following = jnp.minimum(at + 1, blocks - 1)
        into = picked_refs[(block + 1) % GROUP]
        source = picked_refs[block]
        picked = jnp.concatenate(
            [source[pl.ds(chunk, depth, stride=parts), :].astype(jnp.bfloat16) for chunk in range(parts)],
            axis=1,
        )
        gather(following, into, 0, depth // 2)
        turned = dot(jnp.transpose(coupling_ref[block]), picked).astype(jnp.bfloat16)
        projected_ref[block] = jnp.transpose(turned)
        gather(following, into, depth // 2, depth)
        inverse = inverse_ref[...]
        wide = turned.astype(jnp.float32)
        once = wide * inverse
        twice = once * inverse
        once_high, once_low = in_two(once)
        twice_high, twice_low = in_two(twice)
        high = jnp.concatenate([once_high, twice_high], axis=0)
        low = jnp.concatenate([once_low, twice_low], axis=0)
        terms = dot(turned, high, 1, 1) + dot(turned, low, 1, 1)
        spot = spot_ref[at]
        stiff_ref[spot] += terms[:, :width]
        mass_ref[spot] += terms[:, width:]

    @pl.when(step == pl.num_programs(0) - 1)
    def _():
        half = width // 2
        across = lax.broadcasted_iota(jnp.int32, (half, width), 0)
        along = lax.broadcasted_iota(jnp.int32, (half, width), 1)
        for slot in range(SPOTS):
            moved = pltpu.roll(mass_ref[slot, half:, :], half, 1)
            packed_ref[slot, :half, :] = jnp.where(along < across, moved, mass_ref[slot, :half, :])
            diagonal = jnp.sum(jnp.where(along == across, moved, 0.0), axis=0, keepdims=True)
            packed_ref[slot, half:, :] = jnp.broadcast_to(diagonal, (PANEL, width))


def factor_rows(work_ref, rows_ref, first, last):
    width = work_ref.shape[0]

    def panel(at, carry):
        base = pl.multiple_of(at * PANEL, PANEL)
        block = work_ref[pl.ds(base, PANEL), :]
        ahead = pltpu.roll(block[:, :width], width - base, 1)
        entry = {}
        for i in range(PANEL):
            for j in range(i + 1):
                entry[i, j] = jnp.broadcast_to(ahead[j:j + 1, i:i + 1], (1, width))
        rows = [[block[i:i + 1, :width], block[i:i + 1, width:]] for i in range(PANEL)]
        for k in range(PANEL):
            pivot = entry[k, k]
            root = lax.rsqrt(pivot)
            root = root * (1.5 - 0.5 * pivot * root * root)
            for i in range(k + 1, PANEL):
                entry[i, k] = entry[i, k] * root
            rows[k] = [x * root for x in rows[k]]
            for i in range(k + 1, PANEL):
                for j in range(k + 1, i + 1):
                    entry[i, j] = entry[i, j] - entry[i, k] * entry[j, k]
                rows[i] = [x - entry[i, k] * y for x, y in zip(rows[i], rows[k])]
        done = jnp.concatenate(
            [jnp.concatenate([x[0] for x in rows], axis=0), jnp.concatenate([x[1] for x in rows], axis=0)],
            axis=1,
        )
        rows_ref[pl.ds(base, PANEL), :] = done
        high, middle, low = in_three(done)
        left = jnp.concatenate([x[:, :width] for x in (high, high, middle, middle, high, low)], axis=0)
        right = jnp.concatenate([high, middle, high, middle, low, high], axis=0)
        left = jnp.transpose(left).astype(jnp.bfloat16)
        work_ref[...] = work_ref[...] - dot(left, right.astype(jnp.bfloat16))
        return carry

    lax.fori_loop(first // PANEL, last // PANEL, panel, 0)


def exchange_kernel(
    stiff_ref, mass_ref, iface_ref, lumped_ref, reduced_ref, factor_ref, near_ref,
    stiff_in, mass_in, near_in, own_ref, work_ref, rows_ref, send_sem, recv_sem, local_sem,
):
    length = lax.axis_size("sub")
    me = lax.axis_index("sub")
    width = lumped_ref.shape[1]
    half = width // 2
    others = (-3, 3, -2, 2, -1, 1)

    def device(by):
        return lax.rem(me + by + length, length)

    own_mass = pltpu.make_async_copy(mass_ref.at[REACH], mass_in.at[REACH], local_sem.at[0])
    own_stiff = pltpu.make_async_copy(stiff_ref.at[REACH], stiff_in.at[REACH], local_sem.at[1])
    own_mass.start()
    own_stiff.start()
    barrier = pltpu.get_barrier_semaphore()
    for d in others:
        pl.semaphore_signal(barrier, inc=1, device_id={"sub": device(d)}, device_id_type=MESH_ID)
    pl.semaphore_wait(barrier, len(others))

    def send(kind, source, landing, by, slot):
        copy = pltpu.make_async_remote_copy(
            src_ref=source,
            dst_ref=landing,
            send_sem=send_sem.at[kind, slot],
            recv_sem=recv_sem.at[kind, slot],
            device_id={"sub": device(by)},
            device_id_type=MESH_ID,
        )
        copy.start()
        return copy

    mass_copies = [
        send(0, mass_ref.at[d + REACH], mass_in.at[d + REACH], d, d + REACH) for d in others
    ]
    across = lax.broadcasted_iota(jnp.int32, (width, width), 0)
    along = lax.broadcasted_iota(jnp.int32, (width, width), 1)
    own_mass.wait()
    for copy in mass_copies:
        copy.wait_recv()
    stiff_copies = [
        send(1, stiff_ref.at[d + REACH], stiff_in.at[d + REACH], d, d + REACH) for d in others
    ]
    packed = mass_in[REACH]
    for d in others:
        packed = packed + mass_in[d + REACH]
    top = packed[:half]
    low = jnp.concatenate([jnp.zeros_like(top), pltpu.roll(top, half, 1)], axis=0)
    low = jnp.transpose(jnp.where((across >= half) & (along >= half) & (along < across), low, 0.0))
    diagonal = pltpu.roll(packed[half:half + 1], half, 1)
    bottom = jnp.where(across[half:] == along[half:], diagonal, low[half:])
    mass = jnp.concatenate([top, bottom], axis=0)
    work_ref[:, :width] = jnp.where(across == along, mass + lumped_ref[...], mass)
    work_ref[:, width:] = jnp.where(across == along, 1.0, 0.0)
    near_copies = []
    rows = width // PIECES
    for piece in range(PIECES):
        part = pl.ds(piece * rows, rows)
        factor_rows(work_ref, rows_ref, piece * rows, (piece + 1) * rows)
        begun = slice(piece * rows, (piece + 1) * rows)
        own_ref[part, :] = jnp.where(across[begun] >= along[begun], rows_ref[part, width:], 0.0)
        near_copies += [
            send(2 + piece, own_ref.at[part], near_in.at[d + REACH, part], -d, d + REACH) for d in others
        ]
    factor_ref[...] = jnp.transpose(jnp.where(across <= along, rows_ref[:, :width], 0.0))
    own_stiff.wait()
    for copy in stiff_copies:
        copy.wait_recv()
    stiff = stiff_in[REACH]
    for d in others:
        stiff = stiff + stiff_in[d + REACH]
    reduced_ref[...] = iface_ref[0] - stiff
    for copy in mass_copies + stiff_copies:
        copy.wait_send()

    def place(slot, x):
        high, low = in_two(x)
        near_ref[slot, :, :width] = high
        near_ref[slot, :, width:] = low

    place(REACH, own_ref[...])
    for copy in near_copies:
        copy.wait()
    for d in others:
        place(d + REACH, near_in[d + REACH])


def couple_kernel(
    spot_ref, projected_ref, near_ref, reduced_in, factor_in, coupled_ref, reduced_ref, factor_ref
):
    step = pl.program_id(0)

    @pl.when(step == 0)
    def _():
        reduced_ref[0] = reduced_in[...]
        factor_ref[0] = factor_in[...]

    for block in range(GROUP):
        x = projected_ref[block]
        coupled_ref[block] = dot(
            jnp.concatenate([x, x], axis=1), near_ref[spot_ref[step * GROUP + block]], 1, 1
        ).astype(jnp.bfloat16)


def per_device(
    modes, eigenvalues, sub_size, row_offset, stiff_coupling, iface_offset, stiff_iface, lumped_mass
):
    blocks, depth, width = stiff_coupling.shape
    most, count = modes.shape
    f32, bf16 = jnp.float32, jnp.bfloat16
    full = lambda *shape: pl.BlockSpec(shape, lambda i, *_: (0,) * len(shape))
    projected, stiff, mass = pl.pallas_call(
        project_kernel,
        grid_spec=pltpu.PrefetchScalarGridSpec(
            num_scalar_prefetch=2,
            grid=(blocks // GROUP,),
            in_specs=[
                full(blocks, depth),
                full(most, count),
                full(1, count),
                pl.BlockSpec((GROUP, depth, width), lambda i, *_: (i, 0, 0)),
            ],
            out_specs=[
                pl.BlockSpec((GROUP, count, width), lambda i, *_: (i, 0, 0)),
                full(SPOTS, width, width),
                full(SPOTS, width // 2 + PANEL, width),
            ],
            scratch_shapes=[
                pltpu.VMEM((SPOTS, width, width), f32),
                pltpu.VMEM((most * count // width, width), f32),
                pltpu.VMEM((width, count), f32),
                pltpu.VMEM((blocks, depth), jnp.int32),
                pltpu.SMEM((blocks, depth), jnp.int32),
                pltpu.SemaphoreType.DMA,
            ]
            + [pltpu.VMEM((depth * count // width, width), f32)] * GROUP,
        ),
        out_shape=[
            jax.ShapeDtypeStruct((blocks, count, width), bf16),
            jax.ShapeDtypeStruct((SPOTS, width, width), f32),
            jax.ShapeDtypeStruct((SPOTS, width // 2 + PANEL, width), f32),
        ],
        compiler_params=pltpu.CompilerParams(
            dimension_semantics=("arbitrary",), vmem_limit_bytes=20 * MIB
        ),
        name="project",
    )(sub_size, iface_offset, row_offset, modes, eigenvalues, stiff_coupling)

    vmem = pl.BlockSpec(memory_space=pltpu.VMEM)
    reduced, factor, near = pl.pallas_call(
        exchange_kernel,
        in_specs=[pl.BlockSpec(memory_space=pl.ANY)] * 2 + [vmem] * 2,
        out_specs=[vmem] * 3,
        out_shape=[
            jax.ShapeDtypeStruct((width, width), f32),
            jax.ShapeDtypeStruct((width, width), f32),
            jax.ShapeDtypeStruct((SPOTS, width, 2 * width), bf16),
        ],
        scratch_shapes=[
            pltpu.VMEM((SPOTS, width, width), f32),
            pltpu.VMEM((SPOTS, width // 2 + PANEL, width), f32),
            pltpu.VMEM((SPOTS, width, width), f32),
            pltpu.VMEM((width, width), f32),
            pltpu.VMEM((width, 2 * width), f32),
            pltpu.VMEM((width, 2 * width), f32),
            pltpu.SemaphoreType.DMA((2 + PIECES, SPOTS)),
            pltpu.SemaphoreType.DMA((2 + PIECES, SPOTS)),
            pltpu.SemaphoreType.DMA((2,)),
        ],
        compiler_params=pltpu.CompilerParams(
            collective_id=0, has_side_effects=True, vmem_limit_bytes=8 * MIB
        ),
        name="exchange",
    )(stiff, mass, stiff_iface, lumped_mass)

    coupled, reduced, factor = pl.pallas_call(
        couple_kernel,
        grid_spec=pltpu.PrefetchScalarGridSpec(
            num_scalar_prefetch=1,
            grid=(blocks // GROUP,),
            in_specs=[
                pl.BlockSpec((GROUP, count, width), lambda i, *_: (i, 0, 0)),
                full(SPOTS, width, 2 * width),
                full(width, width),
                full(width, width),
            ],
            out_specs=[
                pl.BlockSpec((GROUP, count, width), lambda i, *_: (i, 0, 0)),
                full(1, width, width),
                full(1, width, width),
            ],
        ),
        out_shape=[
            jax.ShapeDtypeStruct((blocks, count, width), bf16),
            jax.ShapeDtypeStruct((1, width, width), f32),
            jax.ShapeDtypeStruct((1, width, width), f32),
        ],
        compiler_params=pltpu.CompilerParams(
            dimension_semantics=("arbitrary",), vmem_limit_bytes=12 * MIB
        ),
        name="couple",
    )(iface_offset, projected, near, reduced, factor)
    return reduced, factor, coupled


def solution(mesh):
    placed = (
        P(("groups", "sub"), None),
        P(("groups", "sub"), None),
        P(("groups", "sub")),
        P(("groups", "sub"), None),
        P(("groups", "sub"), None, None),
        P(("groups", "sub")),
        P(("groups", "sub"), None, None),
        P(("groups", "sub"), None),
    )
    return jax.shard_map(
        per_device,
        mesh=mesh,
        in_specs=placed,
        out_specs=(
            P(("groups", "sub"), None, None),
            P(("groups", "sub"), None, None),
            P(("groups", "sub"), None, None),
        ),
        check_vma=False,
    )
```

```python
import functools

import jax
import jax.numpy as jnp
from jax import lax
from jax.experimental import pallas as pl
from jax.experimental.pallas import tpu as pltpu
from jax.sharding import PartitionSpec as P

REACH = 3
SPOTS = 2 * REACH + 1
GROUP = 4
PANEL = 8
PIECES = 4
MESH_ID = pl.DeviceIdType.MESH
MIB = 1 << 20


def dot(a, b, over_a=1, over_b=0):
    return lax.dot_general(
        a,
        b,
        (((over_a,), (over_b,)), ((), ())),
        preferred_element_type=jnp.float32,
    )


def in_two(x):
    high = x.astype(jnp.bfloat16)
    low = (x - high.astype(jnp.float32)).astype(jnp.bfloat16)
    return high, low


def in_three(x):
    high = x.astype(jnp.bfloat16).astype(jnp.float32)
    middle = (x - high).astype(jnp.bfloat16).astype(jnp.float32)
    return high, middle, x - high - middle


def project_kernel(
    size_ref, spot_ref, offset_ref, modes_ref, eig_ref, coupling_ref,
    projected_ref, stiff_ref, packed_ref, mass_ref, rows_ref, inverse_ref, first_ref, start_ref, sem, *picked_refs,
):
    step = pl.program_id(0)
    depth, width = coupling_ref.shape[1:]
    most, count = modes_ref.shape
    parts = count // width
    blocks = offset_ref.shape[0]

    def gather(at, into, low, high):
        for r in range(low, high):
            into[pl.ds(r * parts, parts), :] = rows_ref[pl.ds(start_ref[at, r], parts), :]

    @pl.when(step == 0)
    def _():
        first_ref[...] = (size_ref[0] - 1 - offset_ref[...]) * parts
        for chunk in range(parts):
            rows_ref[pl.ds(chunk, most, stride=parts), :] = modes_ref[
                :, chunk * width:(chunk + 1) * width
            ].astype(jnp.float32)
            if chunk == 0:
                starts = pltpu.make_async_copy(first_ref, start_ref, sem)
                starts.start()
        inverse_ref[...] = 1.0 / jnp.broadcast_to(eig_ref[...], inverse_ref.shape)
        stiff_ref[...] = jnp.zeros_like(stiff_ref)
        mass_ref[...] = jnp.zeros_like(mass_ref)
        starts.wait()
        gather(0, picked_refs[0], 0, depth)

    for block in range(GROUP):
        at = step * GROUP + block
        following = jnp.minimum(at + 1, blocks - 1)
        into = picked_refs[(block + 1) % GROUP]
        source = picked_refs[block]
        picked = jnp.concatenate(
            [source[pl.ds(chunk, depth, stride=parts), :].astype(jnp.bfloat16) for chunk in range(parts)],
            axis=1,
        )
        gather(following, into, 0, depth // 2)
        turned = dot(jnp.transpose(coupling_ref[block]), picked).astype(jnp.bfloat16)
        projected_ref[block] = jnp.transpose(turned)
        gather(following, into, depth // 2, depth)
        inverse = inverse_ref[...]
        wide = turned.astype(jnp.float32)
        once = wide * inverse
        twice = once * inverse
        once_high, once_low = in_two(once)
        twice_high, twice_low = in_two(twice)
        high = jnp.concatenate([once_high, twice_high], axis=0)
        low = jnp.concatenate([once_low, twice_low], axis=0)
        terms = dot(turned, high, 1, 1) + dot(turned, low, 1, 1)
        spot = spot_ref[at]
        stiff_ref[spot] += terms[:, :width]
        mass_ref[spot] += terms[:, width:]

    @pl.when(step == pl.num_programs(0) - 1)
    def _():
        half = width // 2
        across = lax.broadcasted_iota(jnp.int32, (half, width), 0)
        along = lax.broadcasted_iota(jnp.int32, (half, width), 1)
        for slot in range(SPOTS):
            moved = pltpu.roll(mass_ref[slot, half:, :], half, 1)
            packed_ref[slot, :half, :] = jnp.where(along < across, moved, mass_ref[slot, :half, :])
            diagonal = jnp.sum(jnp.where(along == across, moved, 0.0), axis=0, keepdims=True)
            packed_ref[slot, half:, :] = jnp.broadcast_to(diagonal, (PANEL, width))


def factor_rows(work_ref, rows_ref, first, last):
    width = work_ref.shape[0]

    def panel(at, carry):
        base = pl.multiple_of(at * PANEL, PANEL)
        block = work_ref[pl.ds(base, PANEL), :]
        ahead = pltpu.roll(block[:, :width], width - base, 1)
        entry = {}
        for i in range(PANEL):
            for j in range(i + 1):
                entry[i, j] = jnp.broadcast_to(ahead[j:j + 1, i:i + 1], (1, width))
        rows = [[block[i:i + 1, :width], block[i:i + 1, width:]] for i in range(PANEL)]
        for k in range(PANEL):
            pivot = entry[k, k]
            root = lax.rsqrt(pivot)
            root = root * (1.5 - 0.5 * pivot * root * root)
            for i in range(k + 1, PANEL):
                entry[i, k] = entry[i, k] * root
            rows[k] = [x * root for x in rows[k]]
            for i in range(k + 1, PANEL):
                for j in range(k + 1, i + 1):
                    entry[i, j] = entry[i, j] - entry[i, k] * entry[j, k]
                rows[i] = [x - entry[i, k] * y for x, y in zip(rows[i], rows[k])]
        done = jnp.concatenate(
            [jnp.concatenate([x[0] for x in rows], axis=0), jnp.concatenate([x[1] for x in rows], axis=0)],
            axis=1,
        )
        rows_ref[pl.ds(base, PANEL), :] = done
        high, middle, low = in_three(done)
        left = jnp.concatenate([x[:, :width] for x in (high, high, middle, middle, high, low)], axis=0)
        right = jnp.concatenate([high, middle, high, middle, low, high], axis=0)
        left = jnp.transpose(left).astype(jnp.bfloat16)
        work_ref[...] = work_ref[...] - dot(left, right.astype(jnp.bfloat16))
        return carry

    lax.fori_loop(first // PANEL, last // PANEL, panel, 0)


def exchange_kernel(
    stiff_ref, mass_ref, iface_ref, lumped_ref, reduced_ref, factor_ref, near_ref,
    stiff_in, mass_in, near_in, own_ref, work_ref, rows_ref, send_sem, recv_sem, local_sem,
):
    length = lax.axis_size("sub")
    me = lax.axis_index("sub")
    width = lumped_ref.shape[1]
    half = width // 2
    others = (-3, 3, -2, 2, -1, 1)

    def device(by):
        return lax.rem(me + by + length, length)

    own_mass = pltpu.make_async_copy(mass_ref.at[REACH], mass_in.at[REACH], local_sem.at[0])
    own_stiff = pltpu.make_async_copy(stiff_ref.at[REACH], stiff_in.at[REACH], local_sem.at[1])
    own_mass.start()
    own_stiff.start()
    barrier = pltpu.get_barrier_semaphore()
    for d in others:
        pl.semaphore_signal(barrier, inc=1, device_id={"sub": device(d)}, device_id_type=MESH_ID)
    pl.semaphore_wait(barrier, len(others))

    def send(kind, source, landing, by, slot):
        copy = pltpu.make_async_remote_copy(
            src_ref=source,
            dst_ref=landing,
            send_sem=send_sem.at[kind, slot],
            recv_sem=recv_sem.at[kind, slot],
            device_id={"sub": device(by)},
            device_id_type=MESH_ID,
        )
        copy.start()
        return copy

    mass_copies = [
        send(0, mass_ref.at[d + REACH], mass_in.at[d + REACH], d, d + REACH) for d in others
    ]
    across = lax.broadcasted_iota(jnp.int32, (width, width), 0)
    along = lax.broadcasted_iota(jnp.int32, (width, width), 1)
    own_mass.wait()
    for copy in mass_copies:
        copy.wait_recv()
    stiff_copies = [
        send(1, stiff_ref.at[d + REACH], stiff_in.at[d + REACH], d, d + REACH) for d in others
    ]
    packed = mass_in[REACH]
    for d in others:
        packed = packed + mass_in[d + REACH]
    top = packed[:half]
    low = jnp.concatenate([jnp.zeros_like(top), pltpu.roll(top, half, 1)], axis=0)
    low = jnp.transpose(jnp.where((across >= half) & (along >= half) & (along < across), low, 0.0))
    diagonal = pltpu.roll(packed[half:half + 1], half, 1)
    bottom = jnp.where(across[half:] == along[half:], diagonal, low[half:])
    mass = jnp.concatenate([top, bottom], axis=0)
    work_ref[:, :width] = jnp.where(across == along, mass + lumped_ref[...], mass)
    work_ref[:, width:] = jnp.where(across == along, 1.0, 0.0)
    near_copies = []
    rows = width // PIECES
    for piece in range(PIECES):
        part = pl.ds(piece * rows, rows)
        factor_rows(work_ref, rows_ref, piece * rows, (piece + 1) * rows)
        begun = slice(piece * rows, (piece + 1) * rows)
        own_ref[part, :] = jnp.where(across[begun] >= along[begun], rows_ref[part, width:], 0.0)
        near_copies += [
            send(2 + piece, own_ref.at[part], near_in.at[d + REACH, part], -d, d + REACH) for d in others
        ]
    factor_ref[...] = jnp.transpose(jnp.where(across <= along, rows_ref[:, :width], 0.0))
    own_stiff.wait()
    for copy in stiff_copies:
        copy.wait_recv()
    stiff = stiff_in[REACH]
    for d in others:
        stiff = stiff + stiff_in[d + REACH]
    reduced_ref[...] = iface_ref[0] - stiff
    for copy in mass_copies + stiff_copies:
        copy.wait_send()

    def place(slot, x):
        high, low = in_two(x)
        near_ref[slot, :, :width] = high
        near_ref[slot, :, width:] = low

    place(REACH, own_ref[...])
    for copy in near_copies:
        copy.wait()
    for d in others:
        place(d + REACH, near_in[d + REACH])


def couple_kernel(
    spot_ref, projected_ref, near_ref, reduced_in, factor_in, coupled_ref, reduced_ref, factor_ref
):
    step = pl.program_id(0)

    @pl.when(step == 0)
    def _():
        reduced_ref[0] = reduced_in[...]
        factor_ref[0] = factor_in[...]

    for block in range(GROUP):
        x = projected_ref[block]
        coupled_ref[block] = dot(
            jnp.concatenate([x, x], axis=1), near_ref[spot_ref[step * GROUP + block]], 1, 1
        ).astype(jnp.bfloat16)


def per_device(
    modes, eigenvalues, sub_size, row_offset, stiff_coupling, iface_offset, stiff_iface, lumped_mass
):
    blocks, depth, width = stiff_coupling.shape
    most, count = modes.shape
    f32, bf16 = jnp.float32, jnp.bfloat16
    in_hbm = lambda x: pltpu.with_memory_space_constraint(x, pltpu.HBM)
    full = lambda *shape: pl.BlockSpec(shape, lambda i, *_: (0,) * len(shape))
    projected, stiff, mass = pl.pallas_call(
        project_kernel,
        grid_spec=pltpu.PrefetchScalarGridSpec(
            num_scalar_prefetch=2,
            grid=(blocks // GROUP,),
            in_specs=[
                full(blocks, depth),
                full(most, count),
                full(1, count),
                pl.BlockSpec((GROUP, depth, width), lambda i, *_: (i, 0, 0)),
            ],
            out_specs=[
                pl.BlockSpec((GROUP, count, width), lambda i, *_: (i, 0, 0)),
                full(SPOTS, width, width),
                full(SPOTS, width // 2 + PANEL, width),
            ],
            scratch_shapes=[
                pltpu.VMEM((SPOTS, width, width), f32),
                pltpu.VMEM((most * count // width, width), f32),
                pltpu.VMEM((width, count), f32),
                pltpu.VMEM((blocks, depth), jnp.int32),
                pltpu.SMEM((blocks, depth), jnp.int32),
                pltpu.SemaphoreType.DMA,
            ]
            + [pltpu.VMEM((depth * count // width, width), f32)] * GROUP,
        ),
        out_shape=[
            jax.ShapeDtypeStruct((blocks, count, width), bf16),
            jax.ShapeDtypeStruct((SPOTS, width, width), f32),
            jax.ShapeDtypeStruct((SPOTS, width // 2 + PANEL, width), f32),
        ],
        compiler_params=pltpu.CompilerParams(
            dimension_semantics=("arbitrary",), vmem_limit_bytes=20 * MIB
        ),
        name="project",
    )(sub_size, in_hbm(iface_offset), *map(in_hbm, (row_offset, modes, eigenvalues, stiff_coupling)))

    vmem = pl.BlockSpec(memory_space=pltpu.VMEM)
    reduced, factor, near = pl.pallas_call(
        exchange_kernel,
        in_specs=[pl.BlockSpec(memory_space=pl.ANY)] * 2 + [vmem] * 2,
        out_specs=[vmem] * 3,
        out_shape=[
            jax.ShapeDtypeStruct((width, width), f32),
            jax.ShapeDtypeStruct((width, width), f32),
            jax.ShapeDtypeStruct((SPOTS, width, 2 * width), bf16),
        ],
        scratch_shapes=[
            pltpu.VMEM((SPOTS, width, width), f32),
            pltpu.VMEM((SPOTS, width // 2 + PANEL, width), f32),
            pltpu.VMEM((SPOTS, width, width), f32),
            pltpu.VMEM((width, width), f32),
            pltpu.VMEM((width, 2 * width), f32),
            pltpu.VMEM((width, 2 * width), f32),
            pltpu.SemaphoreType.DMA((2 + PIECES, SPOTS)),
            pltpu.SemaphoreType.DMA((2 + PIECES, SPOTS)),
            pltpu.SemaphoreType.DMA((2,)),
        ],
        compiler_params=pltpu.CompilerParams(
            collective_id=0, has_side_effects=True, vmem_limit_bytes=8 * MIB
        ),
        name="exchange",
    )(stiff, mass, in_hbm(stiff_iface), in_hbm(lumped_mass))

    coupled, reduced, factor = pl.pallas_call(
        couple_kernel,
        grid_spec=pltpu.PrefetchScalarGridSpec(
            num_scalar_prefetch=1,
            grid=(blocks // GROUP,),
            in_specs=[
                pl.BlockSpec((GROUP, count, width), lambda i, *_: (i, 0, 0)),
                full(SPOTS, width, 2 * width),
                full(width, width),
                full(width, width),
            ],
            out_specs=[
                pl.BlockSpec((GROUP, count, width), lambda i, *_: (i, 0, 0)),
                full(1, width, width),
                full(1, width, width),
            ],
        ),
        out_shape=[
            jax.ShapeDtypeStruct((blocks, count, width), bf16),
            jax.ShapeDtypeStruct((1, width, width), f32),
            jax.ShapeDtypeStruct((1, width, width), f32),
        ],
        compiler_params=pltpu.CompilerParams(
            dimension_semantics=("arbitrary",), vmem_limit_bytes=12 * MIB
        ),
        name="couple",
    )(in_hbm(iface_offset), projected, near, reduced, factor)
    return reduced, factor, coupled


def solution(mesh):
    placed = (
        P(("groups", "sub"), None),
        P(("groups", "sub"), None),
        P(("groups", "sub")),
        P(("groups", "sub"), None),
        P(("groups", "sub"), None, None),
        P(("groups", "sub")),
        P(("groups", "sub"), None, None),
        P(("groups", "sub"), None),
    )
    return jax.shard_map(
        per_device,
        mesh=mesh,
        in_specs=placed,
        out_specs=(
            P(("groups", "sub"), None, None),
            P(("groups", "sub"), None, None),
            P(("groups", "sub"), None, None),
        ),
        check_vma=False,
    )
```

```python
import functools

import jax
import jax.numpy as jnp
from jax import lax
from jax.experimental import pallas as pl
from jax.experimental.pallas import tpu as pltpu
from jax.sharding import PartitionSpec as P

REACH = 3
SPOTS = 2 * REACH + 1
GROUP = 4
PANEL = 8
PIECES = 4
MESH_ID = pl.DeviceIdType.MESH
MIB = 1 << 20


def dot(a, b, over_a=1, over_b=0):
    return lax.dot_general(
        a,
        b,
        (((over_a,), (over_b,)), ((), ())),
        preferred_element_type=jnp.float32,
    )


def in_two(x):
    high = x.astype(jnp.bfloat16)
    low = (x - high.astype(jnp.float32)).astype(jnp.bfloat16)
    return high, low


def in_three(x):
    high = x.astype(jnp.bfloat16).astype(jnp.float32)
    middle = (x - high).astype(jnp.bfloat16).astype(jnp.float32)
    return high, middle, x - high - middle


def project_kernel(
    size_ref, spot_ref, offset_ref, modes_ref, eig_ref, coupling_ref,
    projected_ref, stiff_ref, packed_ref, mass_ref, rows_ref, inverse_ref, first_ref, start_ref, sem, *picked_refs,
):
    step = pl.program_id(0)
    depth, width = coupling_ref.shape[1:]
    most, count = modes_ref.shape
    parts = count // width
    blocks = offset_ref.shape[0]

    def gather(at, into, low, high):
        for r in range(low, high):
            into[pl.ds(r * parts, parts), :] = rows_ref[pl.ds(start_ref[at, r], parts), :]

    @pl.when(step == 0)
    def _():
        first_ref[...] = (size_ref[0] - 1 - offset_ref[...]) * parts
        for chunk in range(parts):
            rows_ref[pl.ds(chunk, most, stride=parts), :] = modes_ref[
                :, chunk * width:(chunk + 1) * width
            ].astype(jnp.float32)
            if chunk == 0:
                starts = pltpu.make_async_copy(first_ref, start_ref, sem)
                starts.start()
        inverse_ref[...] = 1.0 / jnp.broadcast_to(eig_ref[...], inverse_ref.shape)
        stiff_ref[...] = jnp.zeros_like(stiff_ref)
        mass_ref[...] = jnp.zeros_like(mass_ref)
        starts.wait()
        gather(0, picked_refs[0], 0, depth)

    for block in range(GROUP):
        at = step * GROUP + block
        following = jnp.minimum(at + 1, blocks - 1)
        into = picked_refs[(block + 1) % GROUP]
        source = picked_refs[block]
        picked = jnp.concatenate(
            [source[pl.ds(chunk, depth, stride=parts), :].astype(jnp.bfloat16) for chunk in range(parts)],
            axis=1,
        )
        gather(following, into, 0, depth // 2)
        turned = dot(jnp.transpose(coupling_ref[block]), picked).astype(jnp.bfloat16)
        projected_ref[block] = jnp.transpose(turned)
        gather(following, into, depth // 2, depth)
        inverse = inverse_ref[...]
        wide = turned.astype(jnp.float32)
        once = wide * inverse
        twice = once * inverse
        once_high, once_low = in_two(once)
        twice_high, twice_low = in_two(twice)
        high = jnp.concatenate([once_high, twice_high], axis=0)
        low = jnp.concatenate([once_low, twice_low], axis=0)
        terms = dot(turned, high, 1, 1) + dot(turned, low, 1, 1)
        spot = spot_ref[at]
        stiff_ref[spot] += terms[:, :width]
        mass_ref[spot] += terms[:, width:]

    @pl.when(step == pl.num_programs(0) - 1)
    def _():
        half = width // 2
        across = lax.broadcasted_iota(jnp.int32, (half, width), 0)
        along = lax.broadcasted_iota(jnp.int32, (half, width), 1)
        for slot in range(SPOTS):
            moved = pltpu.roll(mass_ref[slot, half:, :], half, 1)
            packed_ref[slot, :half, :] = jnp.where(along < across, moved, mass_ref[slot, :half, :])
            diagonal = jnp.sum(jnp.where(along == across, moved, 0.0), axis=0, keepdims=True)
            packed_ref[slot, half:, :] = jnp.broadcast_to(diagonal, (PANEL, width))


def factor_rows(work_ref, rows_ref, first, last):
    width = work_ref.shape[0]

    def panel(at, carry):
        base = pl.multiple_of(at * PANEL, PANEL)
        block = work_ref[pl.ds(base, PANEL), :]
        ahead = pltpu.roll(block[:, :width], width - base, 1)
        entry = {}
        for i in range(PANEL):
            for j in range(i + 1):
                entry[i, j] = jnp.broadcast_to(ahead[j:j + 1, i:i + 1], (1, width))
        rows = [[block[i:i + 1, :width], block[i:i + 1, width:]] for i in range(PANEL)]
        for k in range(PANEL):
            pivot = entry[k, k]
            root = lax.rsqrt(pivot)
            root = root * (1.5 - 0.5 * pivot * root * root)
            for i in range(k + 1, PANEL):
                entry[i, k] = entry[i, k] * root
            rows[k] = [x * root for x in rows[k]]
            for i in range(k + 1, PANEL):
                for j in range(k + 1, i + 1):
                    entry[i, j] = entry[i, j] - entry[i, k] * entry[j, k]
                rows[i] = [x - entry[i, k] * y for x, y in zip(rows[i], rows[k])]
        done = jnp.concatenate(
            [jnp.concatenate([x[0] for x in rows], axis=0), jnp.concatenate([x[1] for x in rows], axis=0)],
            axis=1,
        )
        rows_ref[pl.ds(base, PANEL), :] = done
        high, middle, low = in_three(done)
        left = jnp.concatenate([x[:, :width] for x in (high, high, middle, middle, high, low)], axis=0)
        right = jnp.concatenate([high, middle, high, middle, low, high], axis=0)
        left = jnp.transpose(left).astype(jnp.bfloat16)
        work_ref[...] = work_ref[...] - dot(left, right.astype(jnp.bfloat16))
        return carry

    lax.fori_loop(first // PANEL, last // PANEL, panel, 0)


def exchange_kernel(
    stiff_ref, mass_ref, iface_ref, lumped_ref, reduced_ref, factor_ref, near_ref,
    stiff_in, mass_in, near_in, own_ref, work_ref, rows_ref, send_sem, recv_sem, local_sem,
):
    length = lax.axis_size("sub")
    me = lax.axis_index("sub")
    width = lumped_ref.shape[1]
    half = width // 2
    others = (-3, 3, -2, 2, -1, 1)

    def device(by):
        return lax.rem(me + by + length, length)

    own_mass = pltpu.make_async_copy(mass_ref.at[REACH], mass_in.at[REACH], local_sem.at[0])
    own_stiff = pltpu.make_async_copy(stiff_ref.at[REACH], stiff_in.at[REACH], local_sem.at[1])
    own_mass.start()
    own_stiff.start()
    barrier = pltpu.get_barrier_semaphore()
    for d in others:
        pl.semaphore_signal(barrier, inc=1, device_id={"sub": device(d)}, device_id_type=MESH_ID)
    pl.semaphore_wait(barrier, len(others))

    def send(kind, source, landing, by, slot):
        copy = pltpu.make_async_remote_copy(
            src_ref=source,
            dst_ref=landing,
            send_sem=send_sem.at[kind, slot],
            recv_sem=recv_sem.at[kind, slot],
            device_id={"sub": device(by)},
            device_id_type=MESH_ID,
        )
        copy.start()
        return copy

    mass_copies = [
        send(0, mass_ref.at[d + REACH], mass_in.at[d + REACH], d, d + REACH) for d in others
    ]
    across = lax.broadcasted_iota(jnp.int32, (width, width), 0)
    along = lax.broadcasted_iota(jnp.int32, (width, width), 1)
    own_mass.wait()
    for copy in mass_copies:
        copy.wait_recv()
    stiff_copies = [
        send(1, stiff_ref.at[d + REACH], stiff_in.at[d + REACH], d, d + REACH) for d in others
    ]
    packed = mass_in[REACH]
    for d in others:
        packed = packed + mass_in[d + REACH]
    top = packed[:half]
    low = jnp.concatenate([jnp.zeros_like(top), pltpu.roll(top, half, 1)], axis=0)
    low = jnp.transpose(jnp.where((across >= half) & (along >= half) & (along < across), low, 0.0))
    diagonal = pltpu.roll(packed[half:half + 1], half, 1)
    bottom = jnp.where(across[half:] == along[half:], diagonal, low[half:])
    mass = jnp.concatenate([top, bottom], axis=0)
    work_ref[:, :width] = jnp.where(across == along, mass + lumped_ref[...], mass)
    work_ref[:, width:] = jnp.where(across == along, 1.0, 0.0)
    near_copies = []
    rows = width // PIECES
    for piece in range(PIECES):
        part = pl.ds(piece * rows, rows)
        factor_rows(work_ref, rows_ref, piece * rows, (piece + 1) * rows)
        begun = slice(piece * rows, (piece + 1) * rows)
        own_ref[part, :] = jnp.where(across[begun] >= along[begun], rows_ref[part, width:], 0.0)
        near_copies += [
            send(2 + piece, own_ref.at[part], near_in.at[d + REACH, part], -d, d + REACH) for d in others
        ]
    factor_ref[...] = jnp.transpose(jnp.where(across <= along, rows_ref[:, :width], 0.0))
    own_stiff.wait()
    for copy in stiff_copies:
        copy.wait_recv()
    stiff = stiff_in[REACH]
    for d in others:
        stiff = stiff + stiff_in[d + REACH]
    reduced_ref[...] = iface_ref[0] - stiff
    for copy in mass_copies + stiff_copies:
        copy.wait_send()

    def place(slot, part, x):
        high, low = in_two(x)
        near_ref[slot, part, :width] = high
        near_ref[slot, part, width:] = low

    place(REACH, pl.ds(0, width), own_ref[...])
    for piece in range(PIECES):
        part = pl.ds(piece * rows, rows)
        for d, copy in zip(others, near_copies[piece * len(others):(piece + 1) * len(others)]):
            copy.wait()
            place(d + REACH, part, near_in[d + REACH, part, :])


def couple_kernel(
    spot_ref, projected_ref, near_ref, reduced_in, factor_in, coupled_ref, reduced_ref, factor_ref
):
    step = pl.program_id(0)

    @pl.when(step == 0)
    def _():
        reduced_ref[0] = reduced_in[...]
        factor_ref[0] = factor_in[...]

    for block in range(GROUP):
        x = projected_ref[block]
        coupled_ref[block] = dot(
            jnp.concatenate([x, x], axis=1), near_ref[spot_ref[step * GROUP + block]], 1, 1
        ).astype(jnp.bfloat16)


def per_device(
    modes, eigenvalues, sub_size, row_offset, stiff_coupling, iface_offset, stiff_iface, lumped_mass
):
    blocks, depth, width = stiff_coupling.shape
    most, count = modes.shape
    f32, bf16 = jnp.float32, jnp.bfloat16
    in_hbm = lambda x: pltpu.with_memory_space_constraint(x, pltpu.HBM)
    full = lambda *shape: pl.BlockSpec(shape, lambda i, *_: (0,) * len(shape))
    projected, stiff, mass = pl.pallas_call(
        project_kernel,
        grid_spec=pltpu.PrefetchScalarGridSpec(
            num_scalar_prefetch=2,
            grid=(blocks // GROUP,),
            in_specs=[
                full(blocks, depth),
                full(most, count),
                full(1, count),
                pl.BlockSpec((GROUP, depth, width), lambda i, *_: (i, 0, 0)),
            ],
            out_specs=[
                pl.BlockSpec((GROUP, count, width), lambda i, *_: (i, 0, 0)),
                full(SPOTS, width, width),
                full(SPOTS, width // 2 + PANEL, width),
            ],
            scratch_shapes=[
                pltpu.VMEM((SPOTS, width, width), f32),
                pltpu.VMEM((most * count // width, width), f32),
                pltpu.VMEM((width, count), f32),
                pltpu.VMEM((blocks, depth), jnp.int32),
                pltpu.SMEM((blocks, depth), jnp.int32),
                pltpu.SemaphoreType.DMA,
            ]
            + [pltpu.VMEM((depth * count // width, width), f32)] * GROUP,
        ),
        out_shape=[
            jax.ShapeDtypeStruct((blocks, count, width), bf16),
            jax.ShapeDtypeStruct((SPOTS, width, width), f32),
            jax.ShapeDtypeStruct((SPOTS, width // 2 + PANEL, width), f32),
        ],
        compiler_params=pltpu.CompilerParams(
            dimension_semantics=("arbitrary",), vmem_limit_bytes=20 * MIB
        ),
        name="project",
    )(sub_size, in_hbm(iface_offset), *map(in_hbm, (row_offset, modes, eigenvalues, stiff_coupling)))

    vmem = pl.BlockSpec(memory_space=pltpu.VMEM)
    reduced, factor, near = pl.pallas_call(
        exchange_kernel,
        in_specs=[pl.BlockSpec(memory_space=pl.ANY)] * 2 + [vmem] * 2,
        out_specs=[vmem] * 3,
        out_shape=[
            jax.ShapeDtypeStruct((width, width), f32),
            jax.ShapeDtypeStruct((width, width), f32),
            jax.ShapeDtypeStruct((SPOTS, width, 2 * width), bf16),
        ],
        scratch_shapes=[
            pltpu.VMEM((SPOTS, width, width), f32),
            pltpu.VMEM((SPOTS, width // 2 + PANEL, width), f32),
            pltpu.VMEM((SPOTS, width, width), f32),
            pltpu.VMEM((width, width), f32),
            pltpu.VMEM((width, 2 * width), f32),
            pltpu.VMEM((width, 2 * width), f32),
            pltpu.SemaphoreType.DMA((2 + PIECES, SPOTS)),
            pltpu.SemaphoreType.DMA((2 + PIECES, SPOTS)),
            pltpu.SemaphoreType.DMA((2,)),
        ],
        compiler_params=pltpu.CompilerParams(
            collective_id=0, has_side_effects=True, vmem_limit_bytes=8 * MIB
        ),
        name="exchange",
    )(stiff, mass, in_hbm(stiff_iface), in_hbm(lumped_mass))

    coupled, reduced, factor = pl.pallas_call(
        couple_kernel,
        grid_spec=pltpu.PrefetchScalarGridSpec(
            num_scalar_prefetch=1,
            grid=(blocks // GROUP,),
            in_specs=[
                pl.BlockSpec((GROUP, count, width), lambda i, *_: (i, 0, 0)),
                full(SPOTS, width, 2 * width),
                full(width, width),
                full(width, width),
            ],
            out_specs=[
                pl.BlockSpec((GROUP, count, width), lambda i, *_: (i, 0, 0)),
                full(1, width, width),
                full(1, width, width),
            ],
        ),
        out_shape=[
            jax.ShapeDtypeStruct((blocks, count, width), bf16),
            jax.ShapeDtypeStruct((1, width, width), f32),
            jax.ShapeDtypeStruct((1, width, width), f32),
        ],
        compiler_params=pltpu.CompilerParams(
            dimension_semantics=("arbitrary",), vmem_limit_bytes=12 * MIB
        ),
        name="couple",
    )(in_hbm(iface_offset), projected, near, reduced, factor)
    return reduced, factor, coupled


def solution(mesh):
    placed = (
        P(("groups", "sub"), None),
        P(("groups", "sub"), None),
        P(("groups", "sub")),
        P(("groups", "sub"), None),
        P(("groups", "sub"), None, None),
        P(("groups", "sub")),
        P(("groups", "sub"), None, None),
        P(("groups", "sub"), None),
    )
    return jax.shard_map(
        per_device,
        mesh=mesh,
        in_specs=placed,
        out_specs=(
            P(("groups", "sub"), None, None),
            P(("groups", "sub"), None, None),
            P(("groups", "sub"), None, None),
        ),
        check_vma=False,
    )
```
